32 devices in a mesh: grp: 16 (over z, y, x), ep: 2 (over core).
Axes of the slice: x: 2, y: 2, z: 4, core: 2. Of those that a mesh axis runs over, the one named last changes fastest.
Arguments:
- tokens: bfloat16 [64, 7168], P(('grp', 'ep')), may hold values from -6 to 6
- expert_ids: int32 [64, 8], P(('grp', 'ep')), may hold values from 0 to 15, all different within a row; in each aligned block of 2 rows (0 to 1, 2 to 3, ...) at most 2 rows name the same one
- gate_ints: int32 [64, 8], P(('grp', 'ep')), may hold values from 1 to 16
- w_gate: bfloat16 [16, 7168, 2048], P('grp', None, 'ep'), may hold values from -0.0625 to 0.0625
- w_up: bfloat16 [16, 7168, 2048], P('grp', None, 'ep'), may hold values from -0.0625 to 0.0625
- w_down: bfloat16 [16, 2048, 7168], P('grp', 'ep'), may hold values from -0.125 to 0.125
Outputs:
- mixed: bfloat16 [64, 7168], P(('grp', 'ep'))
The draws below stay inside these ranges and needn't reach their ends.
Inputs may be any that keep to these rules, and one draw needn't show every extreme that they name: `expert_ids`: each row names 8 different experts. Within the 2 rows of one device no expert is named more than 2 times, a bound that some block reaches on some device in every draw.
All inputs are finite; a program needn't handle non-finite values.
Results may differ from the reference program's by a relative error of at most 0.015.
Values may be sent and summed in bfloat16 or wider, within the bound.
A program may use at most 128 MiB of HBM per device.

```python
import math
import jax
import jax.numpy as jnp
import numpy as np
from jax import lax

D = 7168
FF = 2048
TOPK = 8
TOK_DEV = 2
EXPERTS = 16
CAP = 2
TOKENS = 64
DEVICES = 32


def place_ends(values, own_key, least, largest):
    shape = values.shape
    place = [jax.random.randint(jax.random.fold_in(own_key, axis), (), 0, shape[axis]) for axis in range(len(shape))]
    values = values.at[tuple(place)].set(least)
    longest = shape.index(max(shape))
    place[longest] = (place[longest] + 1) % shape[longest]
    return values.at[tuple(place)].set(largest)


def block_levels(rng, dims, cuts, low, top_value):
    factor_of, own = 1.0, jax.random.fold_in(rng, 6)
    for dim, shards_of in cuts:
        steps = jnp.exp(jax.random.uniform(jax.random.fold_in(own, dim), (shards_of,), jnp.float32, low / len(cuts), top_value / len(cuts)))
        factor_of = factor_of * jnp.repeat(steps, dims[dim] // shards_of).reshape([-1 if axis == dim else 1 for axis in range(len(dims))])
    return factor_of


def deal_out(stream_key, own, number, rows, number_of, top, reach, slope):
    sequence = jax.random.permutation(stream_key, number_of)
    heavy_load, common = shares(number_of, rows * top, reach, slope, True), shares(number_of, rows * top, reach, slope, False)
    places = jnp.arange(number_of)

    def named(tallies, turn):
        used = int((tallies > 0).sum())
        fixed = max(1, used // 4)
        moved = fixed + (places - fixed + turn * (used - fixed)) % max(1, number_of - fixed)
        return jnp.zeros((number_of,), jnp.int32).at[sequence[jnp.where(places < fixed, places, moved)]].set(jnp.asarray(tallies, jnp.int32))

    tallies = jnp.where(number % 4 == 0, named(heavy_load, number // 4), named(common, number - number // 4 - 1))
    mixed = jax.random.permutation(jax.random.fold_in(own, 3), number_of)
    giver, sink = mixed[0:number_of // 2 * 2:2], mixed[1:number_of // 2 * 2:2]
    margin = jnp.minimum(tallies[giver] - 1, reach - tallies[sink]) // 2
    margin = jnp.where((giver == sequence[0]) | (sink == sequence[0]) | (tallies[sink] == 0), 0, jnp.maximum(margin, 0))
    moved = jax.random.randint(jax.random.fold_in(own, 4), (number_of // 2,), 0, 1 << 20) % (margin + 1)
    tallies = tallies.at[giver].add(-moved).at[sink].add(moved)
    members = jnp.searchsorted(jnp.cumsum(tallies), jnp.arange(rows * top), side="right").astype(jnp.int32)
    grid = members.reshape(top, rows).T
    grid = grid[jax.random.permutation(jax.random.fold_in(own, 1), rows)]
    turn = jax.random.randint(jax.random.fold_in(own, 2), (rows, 1), 0, top)
    return jnp.take_along_axis(grid, (jnp.arange(top)[None, :] + turn) % top, axis=1)


def shares(count, total, limit, skew, full):
    portions = [(1 << 20) // math.isqrt(rank ** skew) + 1 for rank in range(1, count + 1)]
    largest = limit if full else min(limit, max(-(-total // count), total * portions[0] // sum(portions)))
    least = 1 if total - largest >= count - 1 else 0
    counts, spare = [largest] + [least] * (count - 1), total - largest - least * (count - 1)
    while spare > 0:
        candidates = [i for i in range(1, count) if counts[i] < largest] or [i for i in range(1, count) if counts[i] < limit]
        pool, budget = sum([portions[i] for i in candidates]), spare
        for i in candidates:
            addition = min(limit - counts[i], max(1, budget * portions[i] // pool), spare)
            counts[i] = counts[i] + addition
            spare = spare - addition
    return np.array(counts)


def bell_draw(rng, dims, scale, bound, pieces=(), kind=jnp.bfloat16):
    entries = scale * jax.random.normal(rng, dims, jnp.float32)
    if pieces:
        entries = entries * block_levels(rng, dims, pieces, -0.22, 0.18)
    return jnp.clip(entries, -bound, bound).astype(kind)


def setup_inputs(seed: int = 0) -> dict:
    key_of = jax.random.split(jax.random.key(seed), 7)
    tokens = bell_draw(key_of[0], (TOKENS, D), 1.0, 6.0, ((0, 32),))
    expert_ids_keys = jax.random.split(jax.random.fold_in(key_of[1], 1), TOKENS // TOK_DEV)
    expert_ids_turns = jax.random.permutation(jax.random.fold_in(key_of[1], 3), TOKENS // TOK_DEV)
    expert_ids = jax.vmap(lambda own, number: deal_out(jax.random.fold_in(key_of[1], 2), own, number, TOK_DEV, EXPERTS, TOPK, CAP, 1))(expert_ids_keys, expert_ids_turns).reshape((TOKENS, TOPK))
    gate_ints = place_ends(jax.random.randint(key_of[2], (TOKENS, TOPK), 1, 17), jax.random.fold_in(key_of[2], 1), 1, 16).astype(jnp.int32)
    w_gate = bell_draw(key_of[3], (EXPERTS, D, FF), D ** -0.5, 0.0625, ((0, 16), (2, 2)))
    w_up = bell_draw(key_of[4], (EXPERTS, D, FF), D ** -0.5, 0.0625, ((0, 16), (2, 2)))
    w_down = bell_draw(key_of[5], (EXPERTS, FF, D), FF ** -0.5, 0.125, ((0, 16), (1, 2)))
    return {"tokens": tokens, "expert_ids": expert_ids, "gate_ints": gate_ints, "w_gate": w_gate, "w_up": w_up, "w_down": w_down}


def slot_tables(expert_ids):
    routes = expert_ids.reshape(DEVICES, TOK_DEV * TOPK)
    onehot = (routes[:, :, None] == jnp.arange(EXPERTS, dtype=jnp.int32)[None, None, :]).astype(jnp.int32)
    earlier = jnp.cumsum(onehot, axis=1).astype(jnp.int32) - onehot
    slots = jnp.sum(earlier * onehot, axis=2).astype(jnp.int32)
    return routes, slots


def reference(tokens, expert_ids, gate_ints, w_gate, w_up, w_down):
    routes, slots = slot_tables(expert_ids)
    sources = jnp.arange(DEVICES, dtype=jnp.int32)[:, None]
    token_index = sources * TOK_DEV + jnp.arange(TOK_DEV * TOPK, dtype=jnp.int32)[None, :] // TOPK
    position = (routes * (DEVICES * CAP) + sources * CAP + slots).astype(jnp.int32).reshape(-1)
    table = jnp.zeros((EXPERTS * DEVICES * CAP,), jnp.int32).at[position].set(token_index.reshape(-1).astype(jnp.int32))
    filled = jnp.zeros((EXPERTS * DEVICES * CAP,), jnp.int32).at[position].set(1)
    table = table.reshape(EXPERTS, DEVICES * CAP)
    filled = filled.reshape(EXPERTS, DEVICES * CAP)

    def run_expert(operands):
        row_index, live, gate_w, up_w, down_w = operands
        rows = tokens[row_index] * live.astype(jnp.bfloat16)[:, None]
        gate = jnp.dot(rows, gate_w, preferred_element_type=jnp.float32)
        up = jnp.dot(rows, up_w, preferred_element_type=jnp.float32)
        hidden = (jax.nn.silu(gate) * up).astype(jnp.bfloat16)
        return jnp.dot(hidden, down_w, preferred_element_type=jnp.float32).astype(jnp.bfloat16)

    expert_out = lax.map(run_expert, (table, filled, w_gate, w_up, w_down))
    flat_out = expert_out.reshape(EXPERTS * DEVICES * CAP, D)
    scores = gate_ints.astype(jnp.float32)
    weight = scores / jnp.sum(scores, axis=1, keepdims=True)
    route_rows = position.reshape(TOKENS, TOPK)
    mixed = jnp.zeros((TOKENS, D), jnp.float32)
    for rank in range(TOPK):
        mixed = mixed + weight[:, rank:rank + 1] * flat_out[route_rows[:, rank]].astype(jnp.float32)
    return mixed.astype(jnp.bfloat16)
```

```python
import functools
import jax
import jax.numpy as jnp
from jax import lax
from jax.experimental import pallas as pl
from jax.experimental.pallas import tpu as pltpu
from jax.sharding import PartitionSpec as P

MESH = pl.DeviceIdType.MESH
LANES = 128


def radices_of(count):
    found = []
    rest = count
    if rest % 2 == 0:
        found.append(2)
        rest //= 2
    while rest > 1:
        step = 4 if rest % 4 == 0 else (2 if rest % 2 == 0 else rest)
        found.append(step)
        rest //= step
    return found


def pieces_of(width, most):
    for count in range(most, 0, -1):
        if width % (count * 256) == 0:
            return count
    return 1


def kernel(cfg, tok_ref, ids_ref, gates_ref, wg_hbm, wu_hbm, wd_hbm, out_ref,
           zone, rows, wg, wu, wd, acc_g, acc_u, hid, share, *rest):
    radices, members, chunks, parts = cfg
    stages = len(radices)
    last = stages - 1
    sums = rest[:last]
    sends = rest[last:2 * last]
    recvs = rest[2 * last:3 * last]
    zsum, zsend, zrecv, wsem, gs, gr, rs, rr = rest[3 * last:]
    tok, width = tok_ref.shape
    kc = width // chunks
    nc = width // parts
    me = lax.axis_index("grp") * members + lax.axis_index("ep")
    strides, at = [], 1
    for radix in radices:
        strides.append(at)
        at *= radix
    digit = [lax.rem(lax.div(me, strides[i]), radices[i]) for i in range(stages)]
    span = [1] * last
    for i in range(last - 2, -1, -1):
        span[i] = span[i + 1] * radices[i + 1]

    def other(i, j):
        there = lax.rem(digit[i] + j, radices[i])
        flat = me + (there - digit[i]) * strides[i]
        return there, (lax.div(flat, members), lax.rem(flat, members))

    loads = []
    for c in range(chunks):
        at_k = pl.ds(c * kc, kc)
        loads.append(pltpu.make_async_copy(wg_hbm.at[0, at_k], wg.at[at_k], wsem.at[0, c]))
        loads.append(pltpu.make_async_copy(wu_hbm.at[0, at_k], wu.at[at_k], wsem.at[1, c]))
    downs = []
    for c in range(parts):
        at_n = pl.ds(c * nc, nc)
        downs.append(pltpu.make_async_copy(wd_hbm.at[0, :, at_n], wd.at[:, at_n], wsem.at[2, c]))
    for copy in loads + downs:
        copy.start()

    barrier = pltpu.get_barrier_semaphore()
    peers = 0
    for i in range(stages):
        for j in range(1, radices[i]):
            pl.semaphore_signal(barrier, inc=1, device_id=other(i, j)[1], device_id_type=MESH)
            peers += 1

    lane = lax.broadcasted_iota(jnp.int32, (tok, LANES), 1)
    ids = ids_ref[...]
    scores = gates_ref[...]
    dense = jnp.zeros((tok, LANES), jnp.int32)
    for k in range(ids.shape[1]):
        dense = dense + jnp.where(ids[:, k:k + 1] == lane, scores[:, k:k + 1], 0)
    zone[digit[last], :, pl.ds(0, width)] = tok_ref[...]
    zone[digit[last], :, pl.ds(width, LANES)] = dense.astype(jnp.float32).astype(jnp.bfloat16)
    pl.semaphore_wait(barrier, peers)

    def cols(c):
        return pl.ds(c * kc, kc + (LANES if c == chunks - 1 else 0))

    pending = []

    def push(src, dst, ssem, rsem, dev):
        copy = pltpu.make_async_remote_copy(
            src_ref=src, dst_ref=dst, send_sem=ssem, recv_sem=rsem, device_id=dev, device_id_type=MESH)
        copy.start()
        pending.append(copy)
        return copy

    flight = {}

    def gather_first(c):
        mine = zone.at[digit[last], :, cols(c)]
        flight["g", last, c] = [
            push(mine, mine, gs.at[last, c, j - 1], gr.at[last, c, j - 1], other(last, j)[1])
            for j in range(1, radices[last])]

    def unit_base(i):
        return sum(digit[k] * span[k] for k in range(i + 1))

    def gather_next(c, i):
        for copy in flight["g", i + 1, c]:
            copy.wait_recv()
        if i + 1 == last:
            got = [zone[d, :, cols(c)].astype(jnp.float32) for d in range(radices[last])]
            rows[unit_base(last - 1), :, cols(c)] = jnp.concatenate(got, axis=0).astype(jnp.bfloat16)
        if i >= 0:
            mine = rows.at[pl.ds(unit_base(i), span[i]), :, cols(c)]
            flight["g", i, c] = [
                push(mine, mine, gs.at[i, c, j - 1], gr.at[i, c, j - 1], other(i, j)[1])
                for j in range(1, radices[i])]

    units, unit_rows = rows.shape[0], rows.shape[1]
    total = units * unit_rows

    def up_chunk(c):
        at_k = pl.ds(c * kc, kc)
        loads[2 * c].wait()
        loads[2 * c + 1].wait()
        x = rows[:, :, at_k].astype(jnp.float32).reshape(total, kc).astype(jnp.bfloat16)
        g = jnp.dot(x, wg[at_k, :], preferred_element_type=jnp.float32)
        u = jnp.dot(x, wu[at_k, :], preferred_element_type=jnp.float32)
        if c == 0:
            acc_g[...] = g
            acc_u[...] = u
        else:
            acc_g[...] += g
            acc_u[...] += u

    for c in range(chunks):
        gather_first(c)
    for step in range(chunks + last):
        for i in range(last - 1, -2, -1):
            c = step - (last - 1 - i)
            if 0 <= c < chunks:
                gather_next(c, i)
                if i == -1:
                    up_chunk(c)

    expert = lax.axis_index("grp")
    meta = rows[:, :, pl.ds(width, LANES)].astype(jnp.float32).reshape(total, LANES)
    lanes = lax.broadcasted_iota(jnp.int32, (total, LANES), 1)
    chosen = jnp.sum(jnp.where(lanes == expert, meta, 0.0), axis=1, keepdims=True)
    weight = chosen / jnp.sum(meta, axis=1, keepdims=True)
    share[...] = jnp.broadcast_to(weight, share.shape)
    g = acc_g[...]
    hid[...] = (g / (1.0 + jnp.exp(-g)) * acc_u[...]).astype(jnp.bfloat16)

    def scatter_stage(i, c, value):
        at_n = pl.ds(c * nc, nc)
        value = value.reshape(radices[i], span[i], unit_rows, nc)
        sums[i][c] = value
        sends[i][:, :, :, at_n] = value.astype(jnp.bfloat16)
        copies = []
        for j in range(1, radices[i]):
            there, dev = other(i, j)
            copies.append(push(sends[i].at[there, :, :, at_n], recvs[i].at[j - 1, :, :, at_n],
                               rs.at[i, c, j - 1], rr.at[i, c, j - 1], dev))
        flight["s", i, c] = copies

    def scatter_last(c, value):
        at_n = pl.ds(c * nc, nc)
        value = value.reshape(unit_rows, nc)
        for d in range(radices[last]):
            one = value[d * tok:(d + 1) * tok, :]
            zsum[c, d] = one
            zsend[d, :, at_n] = one.astype(jnp.bfloat16)
        copies = []
        for j in range(1, radices[last]):
            there, dev = other(last, j)
            copies.append(push(zsend.at[there, :, at_n], zrecv.at[j - 1, :, at_n],
                               rs.at[last, c, j - 1], rr.at[last, c, j - 1], dev))
        flight["s", last, c] = copies

    def scatter_step(c, i):
        at_n = pl.ds(c * nc, nc)
        if i == -1:
            downs[c].wait()
            part = jnp.dot(hid[...], wd[:, at_n], preferred_element_type=jnp.float32)
            part = part * share[:, :1]
            scatter_stage(0, c, part)
            return
        for copy in flight["s", i, c]:
            copy.wait_recv()
        if i == last:
            value = zsum[c, digit[last]]
            for j in range(radices[last] - 1):
                value = value + zrecv[j, :, at_n].astype(jnp.float32)
            out_ref[:, at_n] = value.astype(jnp.bfloat16)
            return
        value = sums[i][c, digit[i]]
        for j in range(radices[i] - 1):
            value = value + recvs[i][j, :, :, at_n].astype(jnp.float32)
        if i + 1 == last:
            scatter_last(c, value)
        else:
            scatter_stage(i + 1, c, value)

    for step in range(parts + stages):
        for i in range(-1, stages):
            c = step - (i + 1)
            if 0 <= c < parts:
                scatter_step(c, i)
    for copy in pending:
        copy.wait_send()


def local(cfg, tokens, expert_ids, gate_ints, w_gate, w_up, w_down):
    radices, members, chunks, parts = cfg
    stages = len(radices)
    last = stages - 1
    tok, width = tokens.shape
    hidden = w_gate.shape[2]
    count = 1
    for radix in radices:
        count *= radix
    units = count // radices[last]
    unit_rows = radices[last] * tok
    total = units * unit_rows
    nc = width // parts
    most = max(radices) - 1
    span = [1] * last
    for i in range(last - 2, -1, -1):
        span[i] = span[i + 1] * radices[i + 1]
    bf, f32 = jnp.bfloat16, jnp.float32
    scratch = [
        pltpu.VMEM((radices[last], tok, width + LANES), bf),
        pltpu.VMEM((units, unit_rows, width + LANES), bf),
        pltpu.VMEM((width, hidden), bf),
        pltpu.VMEM((width, hidden), bf),
        pltpu.VMEM((hidden, width), bf),
        pltpu.VMEM((total, hidden), f32),
        pltpu.VMEM((total, hidden), f32),
        pltpu.VMEM((total, hidden), bf),
        pltpu.VMEM((total, LANES), f32),
    ]
    scratch += [pltpu.VMEM((parts, radices[i], span[i], unit_rows, nc), f32) for i in range(last)]
    scratch += [pltpu.VMEM((radices[i], span[i], unit_rows, width), bf) for i in range(last)]
    scratch += [pltpu.VMEM((radices[i] - 1, span[i], unit_rows, width), bf) for i in range(last)]
    scratch += [
        pltpu.VMEM((parts, radices[last], tok, nc), f32),
        pltpu.VMEM((radices[last], tok, width), bf),
        pltpu.VMEM((radices[last] - 1, tok, width), bf),
        pltpu.SemaphoreType.DMA((3, max(chunks, parts))),
        pltpu.SemaphoreType.DMA((stages, chunks, most)),
        pltpu.SemaphoreType.DMA((stages, chunks, most)),
        pltpu.SemaphoreType.DMA((stages, parts, most)),
        pltpu.SemaphoreType.DMA((stages, parts, most)),
    ]
    vmem = pl.BlockSpec(memory_space=pltpu.VMEM)
    hbm = pl.BlockSpec(memory_space=pl.ANY)
    return pl.pallas_call(
        functools.partial(kernel, cfg),
        out_shape=jax.ShapeDtypeStruct((tok, width), bf),
        in_specs=[vmem, vmem, vmem, hbm, hbm, hbm],
        out_specs=vmem,
        scratch_shapes=scratch,
        compiler_params=pltpu.CompilerParams(
            collective_id=0, has_side_effects=True, vmem_limit_bytes=62 * 1024 * 1024),
    )(tokens, expert_ids, gate_ints, w_gate, w_up, w_down)


def solution(mesh):
    count = mesh.shape["grp"] * mesh.shape["ep"]

    def step(tokens, expert_ids, gate_ints, w_gate, w_up, w_down):
        width = tokens.shape[1]
        cfg = (tuple(radices_of(count)), mesh.shape["ep"], pieces_of(width, 4), pieces_of(width, 4))
        return local(cfg, tokens, expert_ids, gate_ints, w_gate, w_up, w_down)

    in_specs = (
        P(("grp", "ep"), None),
        P(("grp", "ep"), None),
        P(("grp", "ep"), None),
        P("grp", None, "ep"),
        P("grp", None, "ep"),
        P("grp", "ep", None),
    )
    out_specs = P(("grp", "ep"), None)
    return jax.shard_map(step, mesh=mesh, in_specs=in_specs, out_specs=out_specs, check_vma=False)
```

```python
import functools
import jax
import jax.numpy as jnp
from jax import lax
from jax.experimental import pallas as pl
from jax.experimental.pallas import tpu as pltpu
from jax.sharding import PartitionSpec as P

MESH = pl.DeviceIdType.MESH
LANES = 128


def radices_of(count):
    found = []
    rest = count
    if rest % 2 == 0:
        found.append(2)
        rest //= 2
    while rest > 1:
        step = 4 if rest % 4 == 0 else (2 if rest % 2 == 0 else rest)
        found.append(step)
        rest //= step
    return found


def pieces_of(width, most):
    for count in range(most, 0, -1):
        if width % (count * 256) == 0:
            return count
    return 1


def kernel(cfg, tok_ref, ids_ref, gates_ref, wg_hbm, wu_hbm, wd_hbm, out_ref,
           zone, rows, wg, wu, wd, acc_g, acc_u, hid, share, *rest):
    radices, members, chunks, parts = cfg
    stages = len(radices)
    last = stages - 1
    sums = rest[:last]
    sends = rest[last:2 * last]
    recvs = rest[2 * last:3 * last]
    zsum, zsend, zrecv, wsem, gs, gr, rs, rr = rest[3 * last:]
    tok, width = tok_ref.shape
    kc = width // chunks
    nc = width // parts
    me = lax.axis_index("grp") * members + lax.axis_index("ep")
    strides, at = [], 1
    for radix in radices:
        strides.append(at)
        at *= radix
    digit = [lax.rem(lax.div(me, strides[i]), radices[i]) for i in range(stages)]
    span = [1] * last
    for i in range(last - 2, -1, -1):
        span[i] = span[i + 1] * radices[i + 1]

    def other(i, j):
        there = lax.rem(digit[i] + j, radices[i])
        flat = me + (there - digit[i]) * strides[i]
        return there, (lax.div(flat, members), lax.rem(flat, members))

    loads = []
    for c in range(chunks):
        at_k = pl.ds(c * kc, kc)
        loads.append(pltpu.make_async_copy(wg_hbm.at[0, at_k], wg.at[at_k], wsem.at[0, c]))
        loads.append(pltpu.make_async_copy(wu_hbm.at[0, at_k], wu.at[at_k], wsem.at[1, c]))
    downs = []
    for c in range(parts):
        at_n = pl.ds(c * nc, nc)
        downs.append(pltpu.make_async_copy(wd_hbm.at[0, :, at_n], wd.at[:, at_n], wsem.at[2, c]))
    for copy in loads + downs:
        copy.start()

    barrier = pltpu.get_barrier_semaphore()
    peers = 0
    for i in range(stages):
        for j in range(1, radices[i]):
            pl.semaphore_signal(barrier, inc=1, device_id=other(i, j)[1], device_id_type=MESH)
            peers += 1

    lane = lax.broadcasted_iota(jnp.int32, (tok, LANES), 1)
    ids = ids_ref[...]
    scores = gates_ref[...]
    dense = jnp.zeros((tok, LANES), jnp.int32)
    for k in range(ids.shape[1]):
        dense = dense + jnp.where(ids[:, k:k + 1] == lane, scores[:, k:k + 1], 0)
    zone[digit[last], :, pl.ds(0, width)] = tok_ref[...]
    zone[digit[last], :, pl.ds(width, LANES)] = dense.astype(jnp.float32).astype(jnp.bfloat16)
    pl.semaphore_wait(barrier, peers)

    def cols(c):
        return pl.ds(c * kc, kc + (LANES if c == chunks - 1 else 0))

    pending = []

    def push(src, dst, ssem, rsem, dev):
        copy = pltpu.make_async_remote_copy(
            src_ref=src, dst_ref=dst, send_sem=ssem, recv_sem=rsem, device_id=dev, device_id_type=MESH)
        copy.start()
        pending.append(copy)
        return copy

    flight = {}

    def gather_first(c):
        mine = zone.at[digit[last], :, cols(c)]
        flight["g", last, c] = [
            push(mine, mine, gs.at[last, c, j - 1], gr.at[last, c, j - 1], other(last, j)[1])
            for j in range(1, radices[last])]

    def unit_base(i):
        return sum(digit[k] * span[k] for k in range(i + 1))

    def gather_next(c, i):
        for copy in flight["g", i + 1, c]:
            copy.wait_recv()
        if i + 1 == last:
            got = [zone[d, :, cols(c)].astype(jnp.float32) for d in range(radices[last])]
            rows[unit_base(last - 1), :, cols(c)] = jnp.concatenate(got, axis=0).astype(jnp.bfloat16)
        if i >= 0:
            mine = rows.at[pl.ds(unit_base(i), span[i]), :, cols(c)]
            flight["g", i, c] = [
                push(mine, mine, gs.at[i, c, j - 1], gr.at[i, c, j - 1], other(i, j)[1])
                for j in range(1, radices[i])]

    units, unit_rows = rows.shape[0], rows.shape[1]
    total = units * unit_rows

    def up_chunk(c):
        at_k = pl.ds(c * kc, kc)
        loads[2 * c].wait()
        loads[2 * c + 1].wait()
        x = rows[:, :, at_k].astype(jnp.float32).reshape(total, kc).astype(jnp.bfloat16)
        g = jnp.dot(x, wg[at_k, :], preferred_element_type=jnp.float32)
        u = jnp.dot(x, wu[at_k, :], preferred_element_type=jnp.float32)
        if c == 0:
            acc_g[...] = g
            acc_u[...] = u
        else:
            acc_g[...] += g
            acc_u[...] += u

    for c in range(chunks):
        gather_first(c)
    for step in range(chunks + last):
        for i in range(last - 1, -2, -1):
            c = step - (last - 1 - i)
            if 0 <= c < chunks:
                gather_next(c, i)
                if i == -1:
                    up_chunk(c)

    expert = lax.axis_index("grp")
    meta = rows[:, :, pl.ds(width, LANES)].astype(jnp.float32).reshape(total, LANES)
    lanes = lax.broadcasted_iota(jnp.int32, (total, LANES), 1)
    chosen = jnp.sum(jnp.where(lanes == expert, meta, 0.0), axis=1, keepdims=True)
    weight = chosen / jnp.sum(meta, axis=1, keepdims=True)
    share[...] = jnp.broadcast_to(weight, share.shape)
    g = acc_g[...]
    hid[...] = (g / (1.0 + jnp.exp(-g)) * acc_u[...]).astype(jnp.bfloat16)

    def scatter_stage(i, c, value):
        at_n = pl.ds(c * nc, nc)
        value = value.reshape(radices[i], span[i], unit_rows, nc)
        sums[i][c] = value
        sends[i][:, :, :, at_n] = value.astype(jnp.bfloat16)
        copies = []
        for j in range(1, radices[i]):
            there, dev = other(i, j)
            copies.append(push(sends[i].at[there, :, :, at_n], recvs[i].at[j - 1, :, :, at_n],
                               rs.at[i, c, j - 1], rr.at[i, c, j - 1], dev))
        flight["s", i, c] = copies

    def scatter_last(c, value):
        at_n = pl.ds(c * nc, nc)
        value = value.reshape(unit_rows, nc)
        for d in range(radices[last]):
            one = value[d * tok:(d + 1) * tok, :]
            zsum[c, d] = one
            zsend[d, :, at_n] = one.astype(jnp.bfloat16)
        copies = []
        for j in range(1, radices[last]):
            there, dev = other(last, j)
            copies.append(push(zsend.at[there, :, at_n], zrecv.at[j - 1, :, at_n],
                               rs.at[last, c, j - 1], rr.at[last, c, j - 1], dev))
        flight["s", last, c] = copies

    def scatter_step(c, i):
        at_n = pl.ds(c * nc, nc)
        if i == -1:
            downs[c].wait()
            part = jnp.dot(hid[...], wd[:, at_n], preferred_element_type=jnp.float32)
            part = part * share[:, :1]
            scatter_stage(0, c, part)
            return
        for copy in flight["s", i, c]:
            copy.wait_recv()
        if i == last:
            value = zsum[c, digit[last]]
            for j in range(radices[last] - 1):
                value = value + zrecv[j, :, at_n].astype(jnp.float32)
            out_ref[:, at_n] = value.astype(jnp.bfloat16)
            return
        value = sums[i][c, digit[i]]
        for j in range(radices[i] - 1):
            value = value + recvs[i][j, :, :, at_n].astype(jnp.float32)
        if i + 1 == last:
            scatter_last(c, value)
        else:
            scatter_stage(i + 1, c, value)

    for step in range(parts + stages):
        for i in range(-1, stages):
            c = step - (i + 1)
            if 0 <= c < parts:
                scatter_step(c, i)
    for copy in pending:
        copy.wait_send()


def local(cfg, tokens, expert_ids, gate_ints, w_gate, w_up, w_down):
    radices, members, chunks, parts = cfg
    stages = len(radices)
    last = stages - 1
    tok, width = tokens.shape
    hidden = w_gate.shape[2]
    count = 1
    for radix in radices:
        count *= radix
    units = count // radices[last]
    unit_rows = radices[last] * tok
    total = units * unit_rows
    nc = width // parts
    most = max(radices) - 1
    span = [1] * last
    for i in range(last - 2, -1, -1):
        span[i] = span[i + 1] * radices[i + 1]
    bf, f32 = jnp.bfloat16, jnp.float32
    scratch = [
        pltpu.VMEM((radices[last], tok, width + LANES), bf),
        pltpu.VMEM((units, unit_rows, width + LANES), bf),
        pltpu.VMEM((width, hidden), bf),
        pltpu.VMEM((width, hidden), bf),
        pltpu.VMEM((hidden, width), bf),
        pltpu.VMEM((total, hidden), f32),
        pltpu.VMEM((total, hidden), f32),
        pltpu.VMEM((total, hidden), bf),
        pltpu.VMEM((total, LANES), f32),
    ]
    scratch += [pltpu.VMEM((parts, radices[i], span[i], unit_rows, nc), f32) for i in range(last)]
    scratch += [pltpu.VMEM((radices[i], span[i], unit_rows, width), bf) for i in range(last)]
    scratch += [pltpu.VMEM((radices[i] - 1, span[i], unit_rows, width), bf) for i in range(last)]
    scratch += [
        pltpu.VMEM((parts, radices[last], tok, nc), f32),
        pltpu.VMEM((radices[last], tok, width), bf),
        pltpu.VMEM((radices[last] - 1, tok, width), bf),
        pltpu.SemaphoreType.DMA((3, max(chunks, parts))),
        pltpu.SemaphoreType.DMA((stages, chunks, most)),
        pltpu.SemaphoreType.DMA((stages, chunks, most)),
        pltpu.SemaphoreType.DMA((stages, parts, most)),
        pltpu.SemaphoreType.DMA((stages, parts, most)),
    ]
    vmem = pl.BlockSpec(memory_space=pltpu.VMEM)
    hbm = pl.BlockSpec(memory_space=pl.ANY)
    return pl.pallas_call(
        functools.partial(kernel, cfg),
        out_shape=jax.ShapeDtypeStruct((tok, width), bf),
        in_specs=[vmem, vmem, vmem, hbm, hbm, hbm],
        out_specs=vmem,
        scratch_shapes=scratch,
        compiler_params=pltpu.CompilerParams(
            collective_id=0, has_side_effects=True, vmem_limit_bytes=62 * 1024 * 1024),
    )(tokens, expert_ids, gate_ints, w_gate, w_up, w_down)


def solution(mesh):
    count = mesh.shape["grp"] * mesh.shape["ep"]

    def step(tokens, expert_ids, gate_ints, w_gate, w_up, w_down):
        width = tokens.shape[1]
        cfg = (tuple(radices_of(count)), mesh.shape["ep"], pieces_of(width, 2), pieces_of(width, 2))
        return local(cfg, tokens, expert_ids, gate_ints, w_gate, w_up, w_down)

    in_specs = (
        P(("grp", "ep"), None),
        P(("grp", "ep"), None),
        P(("grp", "ep"), None),
        P("grp", None, "ep"),
        P("grp", None, "ep"),
        P("grp", "ep", None),
    )
    out_specs = P(("grp", "ep"), None)
    return jax.shard_map(step, mesh=mesh, in_specs=in_specs, out_specs=out_specs, check_vma=False)
```

```python
import functools
import jax
import jax.numpy as jnp
from jax import lax
from jax.experimental import pallas as pl
from jax.experimental.pallas import tpu as pltpu
from jax.sharding import PartitionSpec as P

MESH = pl.DeviceIdType.MESH
LANES = 128


def radices_of(count):
    found = []
    rest = count
    if rest % 2 == 0:
        found.append(2)
        rest //= 2
    while rest > 1:
        step = 4 if rest % 4 == 0 else (2 if rest % 2 == 0 else rest)
        found.append(step)
        rest //= step
    return found


def pieces_of(width, most):
    for count in range(most, 0, -1):
        if width % (count * 256) == 0:
            return count
    return 1


def kernel(cfg, tok_ref, ids_ref, gates_ref, wg_hbm, wu_hbm, wd_hbm, out_ref,
           zone, rows, wg, wu, wd, acc_g, acc_u, hid, share, *rest):
    radices, members, chunks, parts = cfg
    stages = len(radices)
    last = stages - 1
    sums = rest[:last]
    sends = rest[last:2 * last]
    recvs = rest[2 * last:3 * last]
    zsum, zsend, zrecv, wsem, gs, gr, rs, rr = rest[3 * last:]
    tok, width = tok_ref.shape
    kc = width // chunks
    nc = width // parts
    me = lax.axis_index("grp") * members + lax.axis_index("ep")
    strides, at = [], 1
    for radix in radices:
        strides.append(at)
        at *= radix
    digit = [lax.rem(lax.div(me, strides[i]), radices[i]) for i in range(stages)]
    span = [1] * last
    for i in range(last - 2, -1, -1):
        span[i] = span[i + 1] * radices[i + 1]

    def other(i, j):
        there = lax.rem(digit[i] + j, radices[i])
        flat = me + (there - digit[i]) * strides[i]
        return there, (lax.div(flat, members), lax.rem(flat, members))

    loads = []
    for c in range(chunks):
        at_k = pl.ds(c * kc, kc)
        loads.append(pltpu.make_async_copy(wg_hbm.at[0, at_k], wg.at[at_k], wsem.at[0, c]))
        loads.append(pltpu.make_async_copy(wu_hbm.at[0, at_k], wu.at[at_k], wsem.at[1, c]))
    downs = []
    for c in range(parts):
        at_n = pl.ds(c * nc, nc)
        downs.append(pltpu.make_async_copy(wd_hbm.at[0, :, at_n], wd.at[:, at_n], wsem.at[2, c]))
    for copy in loads + downs:
        copy.start()

    barrier = pltpu.get_barrier_semaphore()
    peers = 0
    for i in range(stages):
        for j in range(1, radices[i]):
            pl.semaphore_signal(barrier, inc=1, device_id=other(i, j)[1], device_id_type=MESH)
            peers += 1

    lane = lax.broadcasted_iota(jnp.int32, (tok, LANES), 1)
    ids = ids_ref[...]
    scores = gates_ref[...]
    dense = jnp.zeros((tok, LANES), jnp.int32)
    for k in range(ids.shape[1]):
        dense = dense + jnp.where(ids[:, k:k + 1] == lane, scores[:, k:k + 1], 0)
    zone[digit[last], :, pl.ds(0, width)] = tok_ref[...]
    zone[digit[last], :, pl.ds(width, LANES)] = dense.astype(jnp.float32).astype(jnp.bfloat16)
    pl.semaphore_wait(barrier, peers)

    def cols(c):
        return pl.ds(c * kc, kc + (LANES if c == chunks - 1 else 0))

    pending = []

    def push(src, dst, ssem, rsem, dev):
        copy = pltpu.make_async_remote_copy(
            src_ref=src, dst_ref=dst, send_sem=ssem, recv_sem=rsem, device_id=dev, device_id_type=MESH)
        copy.start()
        pending.append(copy)
        return copy

    flight = {}

    def gather_first(c):
        mine = zone.at[digit[last], :, cols(c)]
        flight["g", last, c] = [
            push(mine, mine, gs.at[last, c, j - 1], gr.at[last, c, j - 1], other(last, j)[1])
            for j in sorted(range(1, radices[last]), key=lambda j: abs(j - 2))]

    def unit_base(i):
        return sum(digit[k] * span[k] for k in range(i + 1))

    def gather_next(c, i):
        for copy in flight["g", i + 1, c]:
            copy.wait_recv()
        if i + 1 == last:
            got = [zone[d, :, cols(c)].astype(jnp.float32) for d in range(radices[last])]
            rows[unit_base(last - 1), :, cols(c)] = jnp.concatenate(got, axis=0).astype(jnp.bfloat16)
        if i >= 0:
            mine = rows.at[pl.ds(unit_base(i), span[i]), :, cols(c)]
            flight["g", i, c] = [
                push(mine, mine, gs.at[i, c, j - 1], gr.at[i, c, j - 1], other(i, j)[1])
                for j in sorted(range(1, radices[i]), key=lambda j: abs(j - 2))]

    units, unit_rows = rows.shape[0], rows.shape[1]
    total = units * unit_rows

    def up_chunk(c):
        at_k = pl.ds(c * kc, kc)
        loads[2 * c].wait()
        loads[2 * c + 1].wait()
        x = rows[:, :, at_k].astype(jnp.float32).reshape(total, kc).astype(jnp.bfloat16)
        g = jnp.dot(x, wg[at_k, :], preferred_element_type=jnp.float32)
        u = jnp.dot(x, wu[at_k, :], preferred_element_type=jnp.float32)
        if c == 0:
            acc_g[...] = g
            acc_u[...] = u
        else:
            acc_g[...] += g
            acc_u[...] += u

    for c in range(chunks):
        gather_first(c)
    for step in range(chunks + last):
        for i in range(last - 1, -2, -1):
            c = step - (last - 1 - i)
            if 0 <= c < chunks:
                gather_next(c, i)
                if i == -1:
                    up_chunk(c)

    expert = lax.axis_index("grp")
    meta = rows[:, :, pl.ds(width, LANES)].astype(jnp.float32).reshape(total, LANES)
    lanes = lax.broadcasted_iota(jnp.int32, (total, LANES), 1)
    chosen = jnp.sum(jnp.where(lanes == expert, meta, 0.0), axis=1, keepdims=True)
    weight = chosen / jnp.sum(meta, axis=1, keepdims=True)
    share[...] = jnp.broadcast_to(weight, share.shape)
    g = acc_g[...]
    hid[...] = (g / (1.0 + jnp.exp(-g)) * acc_u[...]).astype(jnp.bfloat16)

    def scatter_stage(i, c, value):
        at_n = pl.ds(c * nc, nc)
        value = value.reshape(radices[i], span[i], unit_rows, nc)
        sums[i][c] = value
        sends[i][:, :, :, at_n] = value.astype(jnp.bfloat16)
        copies = []
        for j in sorted(range(1, radices[i]), key=lambda j: abs(j - 2)):
            there, dev = other(i, j)
            copies.append(push(sends[i].at[there, :, :, at_n], recvs[i].at[j - 1, :, :, at_n],
                               rs.at[i, c, j - 1], rr.at[i, c, j - 1], dev))
        flight["s", i, c] = copies

    def scatter_last(c, value):
        at_n = pl.ds(c * nc, nc)
        value = value.reshape(unit_rows, nc)
        for d in range(radices[last]):
            one = value[d * tok:(d + 1) * tok, :]
            zsum[c, d] = one
            zsend[d, :, at_n] = one.astype(jnp.bfloat16)
        copies = []
        for j in range(1, radices[last]):
            there, dev = other(last, j)
            copies.append(push(zsend.at[there, :, at_n], zrecv.at[j - 1, :, at_n],
                               rs.at[last, c, j - 1], rr.at[last, c, j - 1], dev))
        flight["s", last, c] = copies

    def scatter_step(c, i):
        at_n = pl.ds(c * nc, nc)
        if i == -1:
            downs[c].wait()
            part = jnp.dot(hid[...], wd[:, at_n], preferred_element_type=jnp.float32)
            part = part * share[:, :1]
            scatter_stage(0, c, part)
            return
        for copy in flight["s", i, c]:
            copy.wait_recv()
        if i == last:
            value = zsum[c, digit[last]]
            for j in range(radices[last] - 1):
                value = value + zrecv[j, :, at_n].astype(jnp.float32)
            out_ref[:, at_n] = value.astype(jnp.bfloat16)
            return
        value = sums[i][c, digit[i]]
        for j in range(radices[i] - 1):
            value = value + recvs[i][j, :, :, at_n].astype(jnp.float32)
        if i + 1 == last:
            scatter_last(c, value)
        else:
            scatter_stage(i + 1, c, value)

    for step in range(parts + stages):
        for i in range(-1, stages):
            c = step - (i + 1)
            if 0 <= c < parts:
                scatter_step(c, i)
    for copy in pending:
        copy.wait_send()


def local(cfg, tokens, expert_ids, gate_ints, w_gate, w_up, w_down):
    radices, members, chunks, parts = cfg
    stages = len(radices)
    last = stages - 1
    tok, width = tokens.shape
    hidden = w_gate.shape[2]
    count = 1
    for radix in radices:
        count *= radix
    units = count // radices[last]
    unit_rows = radices[last] * tok
    total = units * unit_rows
    nc = width // parts
    most = max(radices) - 1
    span = [1] * last
    for i in range(last - 2, -1, -1):
        span[i] = span[i + 1] * radices[i + 1]
    bf, f32 = jnp.bfloat16, jnp.float32
    scratch = [
        pltpu.VMEM((radices[last], tok, width + LANES), bf),
        pltpu.VMEM((units, unit_rows, width + LANES), bf),
        pltpu.VMEM((width, hidden), bf),
        pltpu.VMEM((width, hidden), bf),
        pltpu.VMEM((hidden, width), bf),
        pltpu.VMEM((total, hidden), f32),
        pltpu.VMEM((total, hidden), f32),
        pltpu.VMEM((total, hidden), bf),
        pltpu.VMEM((total, LANES), f32),
    ]
    scratch += [pltpu.VMEM((parts, radices[i], span[i], unit_rows, nc), f32) for i in range(last)]
    scratch += [pltpu.VMEM((radices[i], span[i], unit_rows, width), bf) for i in range(last)]
    scratch += [pltpu.VMEM((radices[i] - 1, span[i], unit_rows, width), bf) for i in range(last)]
    scratch += [
        pltpu.VMEM((parts, radices[last], tok, nc), f32),
        pltpu.VMEM((radices[last], tok, width), bf),
        pltpu.VMEM((radices[last] - 1, tok, width), bf),
        pltpu.SemaphoreType.DMA((3, max(chunks, parts))),
        pltpu.SemaphoreType.DMA((stages, chunks, most)),
        pltpu.SemaphoreType.DMA((stages, chunks, most)),
        pltpu.SemaphoreType.DMA((stages, parts, most)),
        pltpu.SemaphoreType.DMA((stages, parts, most)),
    ]
    vmem = pl.BlockSpec(memory_space=pltpu.VMEM)
    hbm = pl.BlockSpec(memory_space=pl.ANY)
    return pl.pallas_call(
        functools.partial(kernel, cfg),
        out_shape=jax.ShapeDtypeStruct((tok, width), bf),
        in_specs=[vmem, vmem, vmem, hbm, hbm, hbm],
        out_specs=vmem,
        scratch_shapes=scratch,
        compiler_params=pltpu.CompilerParams(
            collective_id=0, has_side_effects=True, vmem_limit_bytes=62 * 1024 * 1024),
    )(tokens, expert_ids, gate_ints, w_gate, w_up, w_down)


def solution(mesh):
    count = mesh.shape["grp"] * mesh.shape["ep"]

    def step(tokens, expert_ids, gate_ints, w_gate, w_up, w_down):
        width = tokens.shape[1]
        cfg = (tuple(radices_of(count)), mesh.shape["ep"], pieces_of(width, 2), pieces_of(width, 2))
        return local(cfg, tokens, expert_ids, gate_ints, w_gate, w_up, w_down)

    in_specs = (
        P(("grp", "ep"), None),
        P(("grp", "ep"), None),
        P(("grp", "ep"), None),
        P("grp", None, "ep"),
        P("grp", None, "ep"),
        P("grp", "ep", None),
    )
    out_specs = P(("grp", "ep"), None)
    return jax.shard_map(step, mesh=mesh, in_specs=in_specs, out_specs=out_specs, check_vma=False)
```
